32 devices in a mesh: tenant: 2 (over x), row: 16 (over z, y, core).
Axes of the slice: x: 2, y: 2, z: 4, core: 2. Of those that a mesh axis runs over, the one named last changes fastest.
Arguments:
- queries: bfloat16 [4096, 256], P(('tenant', 'row')), parts along dimension 0, may hold values from -6 to 6
- probes: int32 [4096, 16], P(('tenant', 'row')), parts along dimension 0, may hold values from 0 to 143, all different within a row; in each aligned block of 128 rows (0 to 127, 128 to 255, ...) at most 32 rows name the same one
- hot_lists: bfloat16 [32, 256, 256], P('tenant'), parts along dimension 0, may hold values from -0.375 to 0.375
- cold_lists: bfloat16 [256, 256, 256], P(('tenant', 'row')), parts along dimension 0, may hold values from -0.375 to 0.375
Outputs:
- nearest: float32 [4096, 128], P(('tenant', 'row')), parts along dimension 0
The draws below stay inside these ranges and needn't reach their ends.
There are 2 independent parts, one for each index of `tenant`. The reference program is written for one: setup_inputs(seed, part) draws one part's arguments, and reference() takes and returns one part's arrays. A program takes and returns all parts, laid end to end along the dimension named above; each array names one. Nothing has to cross between parts.
Inputs may be any that keep to these rules, and one draw needn't show every extreme that they name: `probes`: each query names 16 different lists; every list is named by some query. Within the queries of one index of row (aligned blocks of 128 rows) no list is named more than 32 times, a bound that some block reaches.
All inputs are finite; a program needn't handle non-finite values.
Results may differ from the reference program's by a relative error of at most 0.0003.
Values may be sent and summed in bfloat16 or wider, within the bound.
A program may use at most 64 MiB of HBM per device.

```python
import math
import jax
import jax.numpy as jnp
import numpy as np
from jax import lax

DIM = 256
LSIZE = 256
NPROBE = 16
TOPK = 128
HOT = 16
QDEV = 128
COLD = 128
NLIST = 144
QUERIES = 2048
CAP = 32
N_ROW = 16


def block_levels(stream_key, dims, cuts, low, top_value):
    loudness = 1.0
    for dim, blocks in cuts:
        draws = jax.random.uniform(jax.random.fold_in(jax.random.fold_in(stream_key, 6), dim), (blocks,), jnp.float32, low / len(cuts), top_value / len(cuts))
        loudness = loudness * jnp.repeat(jnp.exp(draws), dims[dim] // blocks).reshape((-1,) + (1,) * (len(dims) - 1 - dim))
    return loudness


def assign_block(key, own, number, rows, count, top, bound, lean):
    order = jax.random.permutation(key, count)
    heavy_load, ordinary = portions_of(count, rows * top, bound, lean, True), portions_of(count, rows * top, bound, lean, False)
    places = jnp.arange(count)

    def named(tallies, rotation):
        used = int((tallies > 0).sum())
        fixed = max(1, used // 4)
        passed = fixed + (places - fixed + rotation * (used - fixed)) % max(1, count - fixed)
        return jnp.zeros((count,), jnp.int32).at[order[jnp.where(places < fixed, places, passed)]].set(jnp.asarray(tallies, jnp.int32))

    tallies = jnp.where(number % 4 == 0, named(heavy_load, number // 4), named(ordinary, number - number // 4 - 1))
    mixed = jax.random.permutation(jax.random.fold_in(own, 3), count)
    donor, receiver = mixed[0:count // 2 * 2:2], mixed[1:count // 2 * 2:2]
    slack = jnp.minimum(tallies[donor] - 1, bound - tallies[receiver]) // 2
    slack = jnp.where((donor == order[0]) | (receiver == order[0]) | (tallies[receiver] == 0), 0, jnp.maximum(slack, 0))
    passed = jax.random.randint(jax.random.fold_in(own, 4), (count // 2,), 0, 1 << 20) % (slack + 1)
    tallies = tallies.at[donor].add(-passed).at[receiver].add(passed)
    members = jnp.searchsorted(jnp.cumsum(tallies), jnp.arange(rows * top), side="right").astype(jnp.int32)
    grid = members.reshape(top, rows).T
    grid = grid[jax.random.permutation(jax.random.fold_in(own, 1), rows)]
    rotation = jax.random.randint(jax.random.fold_in(own, 2), (rows, 1), 0, top)
    return jnp.take_along_axis(grid, (jnp.arange(top)[None, :] + rotation) % top, axis=1)


def portions_of(amount, total, bound, skew, full):
    portions = [(1 << 20) // math.isqrt(standing ** skew) + 1 for standing in range(1, amount + 1)]
    largest = bound if full else min(bound, max(-(-total // amount), total * portions[0] // sum(portions)))
    least = 1 if total - largest >= amount - 1 else 0
    counts, rest = [largest] + [least] * (amount - 1), total - largest - least * (amount - 1)
    while rest > 0:
        movable = [i for i in range(1, amount) if counts[i] < largest] or [i for i in range(1, amount) if counts[i] < bound]
        mass, remaining = sum([portions[i] for i in movable]), rest
        for i in movable:
            more = min(bound - counts[i], max(1, remaining * portions[i] // mass), rest)
            counts[i] = counts[i] + more
            rest = rest - more
    return np.array(counts)


def scatter_about(rng, shape, width, limit, pieces=(), kind=jnp.bfloat16):
    array = width * jax.random.normal(rng, shape, jnp.float32)
    if pieces:
        array = array * block_levels(rng, shape, pieces, -0.22, 0.18)
    return jnp.clip(array, -limit, limit).astype(kind)


def setup_inputs(seed: int = 0, part: int = 0) -> dict:
    key_list = jax.random.split(jax.random.key(seed), 5)
    part_keys = jax.random.split(jax.random.fold_in(key_list[4], part), 5)
    queries = scatter_about(part_keys[0], (QUERIES, DIM), 1.0, 6.0, ((0, 16),))
    probes_keys = jax.random.split(jax.random.fold_in(part_keys[1], 1), QUERIES // QDEV)
    probes_turns = jax.random.permutation(jax.random.fold_in(part_keys[1], 3), QUERIES // QDEV)
    probes = jax.vmap(lambda own, number: assign_block(jax.random.fold_in(part_keys[1], 2), own, number, QDEV, NLIST, NPROBE, CAP, 2))(probes_keys, probes_turns).reshape((QUERIES, NPROBE))
    hot_lists = scatter_about(part_keys[2], (HOT, LSIZE, DIM), DIM ** -0.5, 0.375)
    cold_lists = scatter_about(part_keys[3], (COLD, LSIZE, DIM), DIM ** -0.5, 0.375, ((0, 16),))
    return {"queries": queries, "probes": probes, "hot_lists": hot_lists, "cold_lists": cold_lists}


def reference(queries, probes, hot_lists, cold_lists):
    lists = jnp.concatenate([hot_lists, cold_lists], axis=0)
    flat = probes.reshape(-1).astype(jnp.int32)
    count = flat.shape[0]
    pair_query = (jnp.arange(count, dtype=jnp.int32) // NPROBE).astype(jnp.int32)
    source = (pair_query // QDEV).astype(jnp.int32)
    keys = source * NLIST + flat
    order = jnp.argsort(keys, stable=True).astype(jnp.int32)
    sorted_keys = keys[order]
    position = jnp.zeros((count,), jnp.int32).at[order].set(jnp.arange(count, dtype=jnp.int32))
    first = jnp.searchsorted(sorted_keys, keys, side="left").astype(jnp.int32)
    column = source * CAP + (position - first)
    span = N_ROW * CAP
    table = jnp.zeros((NLIST * span,), jnp.int32).at[flat * span + column].set(pair_query)
    table = table.reshape(NLIST, span)
    group = 16
    blocks = (NLIST + group - 1) // group
    padding = blocks * group - NLIST
    lists_pad = jnp.pad(lists, ((0, padding), (0, 0), (0, 0))).reshape(blocks, group, LSIZE, DIM)
    table_pad = jnp.pad(table, ((0, padding), (0, 0))).reshape(blocks, group, span)

    def one_block(pair):
        group_lists, group_table = pair
        gathered = queries[group_table].astype(jnp.float32)
        scores = jnp.einsum("lwd,lvd->lwv", gathered, group_lists.astype(jnp.float32),
                            precision=lax.Precision.HIGHEST)
        return lax.top_k(scores, TOPK)[0]

    best = lax.map(one_block, (lists_pad, table_pad)).reshape(blocks * group, span, TOPK)
    candidates = best[flat, column].reshape(QUERIES, NPROBE * TOPK)
    return lax.top_k(candidates, TOPK)[0]
```

```python
import functools
import math

import jax
import jax.numpy as jnp
from jax import lax
from jax.experimental import pallas as pl
from jax.experimental.pallas import tpu as pltpu
from jax.sharding import PartitionSpec as P

TOPK = 128
LOW = -3.0e38
SUB = 8
LANES = 128


def hot_scores(queries, hot_lists):
    hot_count, lsize, width = hot_lists.shape
    qcount = queries.shape[0]
    flat_hot = hot_lists.reshape(hot_count * lsize, width)
    scores = lax.dot_general(
        queries, flat_hot, (((1,), (1,)), ((), ())), preferred_element_type=jnp.float32
    )
    return scores.reshape(qcount, hot_count, lsize)


def earlier_equal(flat):
    count = flat.shape[0]
    block = math.gcd(count, 512)
    index_all = jnp.arange(count, dtype=jnp.int32)

    def one_block(start):
        ids = lax.dynamic_slice_in_dim(flat, start, block, 0)
        where_at = start + jnp.arange(block, dtype=jnp.int32)
        same = (ids[:, None] == flat[None, :]) & (index_all[None, :] < where_at[:, None])
        return jnp.sum(same.astype(jnp.int32), axis=1)

    starts = jnp.arange(count // block, dtype=jnp.int32) * block
    return lax.map(one_block, starts).reshape(count)


def general(queries, probes, hot_lists, cold_lists):
    rows = lax.axis_size("row")
    qcount, nprobe = probes.shape
    list_dev = cold_lists.shape[0]
    hot_count, lsize, width = hot_lists.shape
    capacity = 2 * ((qcount * nprobe + list_dev * rows - 1) // (list_dev * rows))
    total = rows * list_dev * capacity
    flat = probes.reshape(-1)
    count = flat.shape[0]
    pair_query = jnp.arange(count, dtype=jnp.int32) // nprobe
    rank = earlier_equal(flat)
    cold_id = flat - hot_count
    is_cold = cold_id >= 0
    slot = jnp.where(is_cold, cold_id * capacity + rank, total)
    outgoing = (
        jnp.zeros((total, width), jnp.bfloat16).at[slot].set(queries[pair_query], mode="drop")
    )
    outgoing = outgoing.reshape(rows, list_dev, capacity, width)
    arrived = lax.all_to_all(outgoing, "row", split_axis=0, concat_axis=0, tiled=True)
    scores = jnp.einsum("slcd,lvd->slcv", arrived, cold_lists, preferred_element_type=jnp.float32)
    reading = jnp.minimum(slot, total - 1)
    returned = lax.all_to_all(scores, "row", split_axis=0, concat_axis=0, tiled=True).reshape(
        total, lsize
    )
    cold_rows = returned[reading]
    hot_all = hot_scores(queries, hot_lists)
    hot_pick = jnp.clip(probes, 0, hot_count - 1)
    hot_rows = jnp.take_along_axis(hot_all, hot_pick[:, :, None], axis=1).reshape(count, lsize)
    merged = jnp.where(is_cold[:, None], cold_rows, hot_rows).reshape(qcount, nprobe * lsize)
    return lax.top_k(merged, TOPK)[0]


def batcher(n):
    pairs = []
    p = 1
    while p < n:
        k = p
        while k >= 1:
            for j in range(k % p, n - k, 2 * k):
                for i in range(min(k, n - j - k)):
                    if (i + j) // (2 * p) == (i + j + k) // (2 * p):
                        pairs.append((i + j, i + j + k))
            k //= 2
        p *= 2
    return pairs


def exchange(vals, a, b):
    x, y = vals[a], vals[b]
    vals[a], vals[b] = jnp.maximum(x, y), jnp.minimum(x, y)


def clean(vals, where, dists):
    for d in dists:
        for i in range(len(where)):
            if i & d == 0:
                exchange(vals, where[i], where[i + d])


def at(i):
    return pl.ds(pl.multiple_of(i * SUB, SUB), SUB)


def loop(n, unroll, body):
    @pl.loop(0, n // unroll)
    def _(step):
        for u in range(unroll):
            body(step * unroll + u)


def sort_runs(ref, count):
    net = batcher(32)

    def body(t):
        vals = [ref[at(t * 32 + i), :] for i in range(32)]
        for a, b in net:
            exchange(vals, a, b)
        for i in range(32):
            ref[at(t * 32 + i), :] = vals[i]

    loop(count // 32, 1, body)


def join_runs(ref, count, half):
    size = 2 * half
    step = half // 4
    per = 4

    @pl.loop(0, count // size * step // per)
    def _(t):
        base = t * per // step * size
        first = t * per % step
        work = []
        for u in range(per):
            i = first + u
            idx = [base + i + step * k for k in range(4)]
            idx += [base + size - 1 - i - step * k for k in range(4)]
            work.append((idx, [ref[at(x), :] for x in idx]))
        for _, vals in work:
            for k in range(4):
                exchange(vals, k, 4 + k)
            clean(vals, [0, 1, 2, 3], (2, 1))
            clean(vals, [7, 6, 5, 4], (2, 1))
        for idx, vals in work:
            for x, v in zip(idx, vals):
                ref[at(x), :] = v

    tidy(ref, ref, count, step)


def tidy(src, dst, count, block):
    dists = []
    d = block // 2
    while d:
        dists.append(d)
        d //= 2

    @pl.loop(0, count // 32)
    def _(t):
        vals = [src[at(t * 32 + i), :] for i in range(32)]
        for c in range(32 // block):
            clean(vals, list(range(c * block, (c + 1) * block)), dists)
        for i in range(32):
            dst[at(t * 32 + i), :] = vals[i]


def best_of(a, abase, b, bbase, tmp, dst, turn=0):
    step = TOPK // 8
    per = 2

    @pl.loop(0, step // per)
    def _(t):
        work = []
        for u in range(per):
            i = t * per + u
            vals = []
            for k in range(8):
                x = a[at(abase + i + step * k), :]
                y = b[at(bbase + TOPK - 1 - i - step * k), :]
                if turn:
                    y = pltpu.roll(y, turn, 0)
                vals.append(jnp.maximum(x, y))
            work.append(vals)
        for vals in work:
            clean(vals, list(range(8)), (4, 2, 1))
        for u, vals in enumerate(work):
            for k in range(8):
                tmp[at(t * per + u + step * k), :] = vals[k]

    tidy(tmp, dst, TOPK, step)


def fused(
    rows, cap, q_ref, pt_ref, hot_ref, cold_ref, out_ref,
    q_all, pt_all, key, onehot, work, short, tmp, runs, hotbest, sendbuf, recv,
    qs_sem, qr_sem, ps_sem, pr_sem, ss_sem, sr_sem,
):
    me = lax.axis_index("row")
    qcount = q_ref.shape[0]
    hot_count, lsize = hot_ref.shape[0], hot_ref.shape[1]
    list_dev = cold_ref.shape[0]
    nprobe = pt_ref.shape[0]
    pack = LANES // cap
    f32 = jnp.float32

    def peer(b):
        return {"row": b}

    def q_copy(b, slot):
        return pltpu.make_async_remote_copy(
            src_ref=q_ref, dst_ref=q_all.at[slot], send_sem=qs_sem.at[b], recv_sem=qr_sem.at[slot],
            device_id=peer(b), device_id_type=pl.DeviceIdType.MESH,
        )

    def p_copy(b, slot):
        return pltpu.make_async_remote_copy(
            src_ref=pt_ref, dst_ref=pt_all.at[slot], send_sem=ps_sem.at[b], recv_sem=pr_sem.at[slot],
            device_id=peer(b), device_id_type=pl.DeviceIdType.MESH,
        )

    def s_copy(b, slot):
        return pltpu.make_async_remote_copy(
            src_ref=sendbuf.at[b], dst_ref=recv.at[slot], send_sem=ss_sem.at[b],
            recv_sem=sr_sem.at[slot], device_id=peer(b), device_id_type=pl.DeviceIdType.MESH,
        )

    barrier = pltpu.get_barrier_semaphore()

    @pl.loop(1, rows)
    def _(d):
        pl.semaphore_signal(
            barrier, inc=1, device_id=peer(lax.rem(me + d, rows)), device_id_type=pl.DeviceIdType.MESH
        )

    pl.semaphore_wait(barrier, rows - 1)

    @pl.loop(1, rows)
    def _(d):
        b = lax.rem(me + d, rows)
        p_copy(b, me).start()
        q_copy(b, me).start()

    q_all[me] = q_ref[...]
    pt_all[me] = pt_ref[...]

    before = (
        lax.broadcasted_iota(jnp.int32, (qcount, qcount), 0)
        < lax.broadcasted_iota(jnp.int32, (qcount, qcount), 1)
    )
    before = jnp.where(before, 1.0, 0.0).astype(jnp.bfloat16)

    def keys_of(pt, first, count):
        ids = first + lax.broadcasted_iota(jnp.int32, (count, qcount), 0)
        named = pt[0:1, :] == ids
        for j in range(1, nprobe):
            named = named | (pt[j : j + 1, :] == ids)
        ones = jnp.where(named, 1.0, 0.0)
        rank = jnp.dot(ones.astype(jnp.bfloat16), before, preferred_element_type=f32)
        return named, rank

    slot_row = lax.broadcasted_iota(jnp.int32, (LANES, pack * qcount), 0).astype(f32)
    lane = lax.broadcasted_iota(jnp.int32, (lsize, LANES), 1)

    def match(l):
        hit = slot_row == key[l : l + 1, :]
        hot1 = jnp.where(hit, 1.0, 0.0).astype(jnp.bfloat16)
        onehot[l] = hot1
        return hot1

    def spread(l, half):
        part = short[pl.ds(l, TOPK, stride=SUB), :]
        high = part.astype(jnp.bfloat16)
        low = (part - high.astype(f32)).astype(jnp.bfloat16)
        hot1 = onehot[l]
        full = jnp.dot(high, hot1, preferred_element_type=f32)
        full = full + jnp.dot(low, hot1, preferred_element_type=f32)
        full = jnp.where(key[l : l + 1, :] >= 0.0, full, LOW)
        for b in range(pack):
            runs[l // half, pl.ds((l % half) * pack + b, TOPK, stride=SUB), :] = full[
                :, b * qcount : (b + 1) * qcount
            ]

    def shorten():
        sort_runs(work, lsize)
        join_runs(work, lsize, 32)
        join_runs(work, lsize, 64)
        best_of(work, 0, work, TOPK, tmp, short)

    half = SUB // pack

    named, rank = keys_of(pt_ref[...], 0, hot_count)
    for l in range(hot_count):
        value = jnp.where(named[l : l + 1, :], rank[l : l + 1, :] + float(cap * (l % pack)), -1.0)
        key[l // pack : l // pack + 1, (l % pack) * qcount : (l % pack + 1) * qcount] = value
    mine = q_ref[...]
    stack = jnp.concatenate([mine] * pack, axis=0)
    for t in range(hot_count // pack):
        rows_t = jnp.dot(match(t), stack, preferred_element_type=f32).astype(jnp.bfloat16)
        score = None
        for c in range(pack):
            one = lax.dot_general(
                hot_ref[t * pack + c], rows_t, (((1,), (1,)), ((), ())), preferred_element_type=f32
            )
            score = one if score is None else jnp.where(lane >= c * cap, one, score)
        work[pl.ds(t, lsize, stride=SUB), :] = score
        if hot_count // pack + t < SUB:
            work[pl.ds(hot_count // pack + t, lsize, stride=SUB), :] = score
    shorten()
    for t in range(hot_count // pack):
        spread(t, half)
    best_of(runs.at[0], 0, runs.at[1], 0, tmp, hotbest)

    groups = rows // pack

    @pl.loop(0, groups)
    def _(step):
        g = lax.rem(me // pack + 1 + step, groups)
        for b in range(pack):
            block = g * pack + b

            @pl.when(block != me)
            def _():
                p_copy(block, block).wait_recv()
                q_copy(block, block).wait_recv()

            named, rank = keys_of(pt_all[block], hot_count + me * list_dev, list_dev)
            key[:, b * qcount : (b + 1) * qcount] = jnp.where(named, rank + float(cap * b), -1.0)
        stack = q_all[pl.ds(g * pack, pack)].reshape(pack * qcount, q_ref.shape[1])
        for l in range(list_dev):
            rows_l = jnp.dot(match(l), stack, preferred_element_type=f32).astype(jnp.bfloat16)
            work[pl.ds(l, lsize, stride=SUB), :] = lax.dot_general(
                cold_ref[l], rows_l, (((1,), (1,)), ((), ())), preferred_element_type=f32
            )
        shorten()
        for l in range(list_dev):
            spread(l, half)
        best_of(runs.at[0], 0, runs.at[1], 0, tmp, runs.at[0])
        best_of(runs.at[2], 0, runs.at[3], 0, tmp, runs.at[2])
        best_of(runs.at[0], 0, runs.at[2], 0, tmp, runs.at[0])
        best_of(runs.at[0], 0, runs.at[0], 0, tmp, runs.at[1], turn=pack)
        for b in range(pack):
            block = g * pack + b
            sendbuf[block] = runs[1, pl.ds(b, TOPK, stride=SUB), :]

            @pl.when(block != me)
            def _():
                s_copy(block, me).start()

    recv[me] = sendbuf[me]

    @pl.loop(1, rows)
    def _(d):
        b = lax.rem(me + d, rows)
        s_copy(b, b).wait_recv()

    for o in range(rows):
        runs[o // SUB, pl.ds(o % SUB, TOPK, stride=SUB), :] = recv[o]
    for k in range(rows // SUB):
        best_of(hotbest, 0, runs.at[k], 0, tmp, hotbest)
    turn = SUB // 2
    src, dst = hotbest, runs.at[0]
    while turn:
        best_of(src, 0, src, 0, tmp, dst, turn=turn)
        src, dst = dst, src
        turn //= 2
    result = src[pl.ds(0, TOPK, stride=SUB), :]
    out_ref[...] = result.T

    @pl.loop(1, rows)
    def _(d):
        b = lax.rem(me + d, rows)
        p_copy(b, me).wait_send()
        q_copy(b, me).wait_send()
        s_copy(b, me).wait_send()


def shards(queries, probes, hot_lists, cold_lists):
    rows = lax.axis_size("row")
    qcount, nprobe = probes.shape
    list_dev = cold_lists.shape[0]
    hot_count, lsize, width = hot_lists.shape
    cap = 2 * ((qcount * nprobe + list_dev * rows - 1) // (list_dev * rows))
    pack = LANES // cap
    fits = (
        qcount == LANES and lsize == 2 * TOPK and list_dev == SUB and pack == 4
        and hot_count == pack * pack and rows == 2 * SUB
    )
    if not fits:
        return general(queries, probes, hot_lists, cold_lists)
    vmem = pl.BlockSpec(memory_space=pltpu.VMEM)
    dma = pltpu.SemaphoreType.DMA((rows,))
    return pl.pallas_call(
        functools.partial(fused, rows, cap),
        out_shape=jax.ShapeDtypeStruct((qcount, TOPK), jnp.float32),
        in_specs=[vmem] * 4,
        out_specs=vmem,
        scratch_shapes=[
            pltpu.VMEM((rows, qcount, width), jnp.bfloat16),
            pltpu.VMEM((rows, nprobe, qcount), jnp.int32),
            pltpu.VMEM((list_dev, pack * qcount), jnp.float32),
            pltpu.VMEM((list_dev, LANES, pack * qcount), jnp.bfloat16),
            pltpu.VMEM((lsize * SUB, LANES), jnp.float32),
            pltpu.VMEM((TOPK * SUB, LANES), jnp.float32),
            pltpu.VMEM((TOPK * SUB, LANES), jnp.float32),
            pltpu.VMEM((list_dev * pack // SUB, TOPK * SUB, LANES), jnp.float32),
            pltpu.VMEM((TOPK * SUB, LANES), jnp.float32),
            pltpu.VMEM((rows, TOPK, qcount), jnp.float32),
            pltpu.VMEM((rows, TOPK, qcount), jnp.float32),
            dma, dma, dma, dma, dma, dma,
        ],
        compiler_params=pltpu.CompilerParams(
            collective_id=0, has_side_effects=True, vmem_limit_bytes=48 * 1024 * 1024
        ),
    )(queries, probes.T, hot_lists, cold_lists)


def solution(mesh):
    placed = (
        P(("tenant", "row"), None),
        P(("tenant", "row"), None),
        P("tenant", None, None),
        P(("tenant", "row"), None, None),
    )
    return jax.shard_map(
        shards, mesh=mesh, in_specs=placed, out_specs=P(("tenant", "row"), None), check_vma=False
    )
```

```python
import functools
import math

import jax
import jax.numpy as jnp
from jax import lax
from jax.experimental import pallas as pl
from jax.experimental.pallas import tpu as pltpu
from jax.sharding import PartitionSpec as P

TOPK = 128
LOW = -3.0e38
SUB = 8
LANES = 128


def hot_scores(queries, hot_lists):
    hot_count, lsize, width = hot_lists.shape
    qcount = queries.shape[0]
    flat_hot = hot_lists.reshape(hot_count * lsize, width)
    scores = lax.dot_general(
        queries, flat_hot, (((1,), (1,)), ((), ())), preferred_element_type=jnp.float32
    )
    return scores.reshape(qcount, hot_count, lsize)


def earlier_equal(flat):
    count = flat.shape[0]
    block = math.gcd(count, 512)
    index_all = jnp.arange(count, dtype=jnp.int32)

    def one_block(start):
        ids = lax.dynamic_slice_in_dim(flat, start, block, 0)
        where_at = start + jnp.arange(block, dtype=jnp.int32)
        same = (ids[:, None] == flat[None, :]) & (index_all[None, :] < where_at[:, None])
        return jnp.sum(same.astype(jnp.int32), axis=1)

    starts = jnp.arange(count // block, dtype=jnp.int32) * block
    return lax.map(one_block, starts).reshape(count)


def general(queries, probes, hot_lists, cold_lists):
    rows = lax.axis_size("row")
    qcount, nprobe = probes.shape
    list_dev = cold_lists.shape[0]
    hot_count, lsize, width = hot_lists.shape
    capacity = 2 * ((qcount * nprobe + list_dev * rows - 1) // (list_dev * rows))
    total = rows * list_dev * capacity
    flat = probes.reshape(-1)
    count = flat.shape[0]
    pair_query = jnp.arange(count, dtype=jnp.int32) // nprobe
    rank = earlier_equal(flat)
    cold_id = flat - hot_count
    is_cold = cold_id >= 0
    slot = jnp.where(is_cold, cold_id * capacity + rank, total)
    outgoing = (
        jnp.zeros((total, width), jnp.bfloat16).at[slot].set(queries[pair_query], mode="drop")
    )
    outgoing = outgoing.reshape(rows, list_dev, capacity, width)
    arrived = lax.all_to_all(outgoing, "row", split_axis=0, concat_axis=0, tiled=True)
    scores = jnp.einsum("slcd,lvd->slcv", arrived, cold_lists, preferred_element_type=jnp.float32)
    reading = jnp.minimum(slot, total - 1)
    returned = lax.all_to_all(scores, "row", split_axis=0, concat_axis=0, tiled=True).reshape(
        total, lsize
    )
    cold_rows = returned[reading]
    hot_all = hot_scores(queries, hot_lists)
    hot_pick = jnp.clip(probes, 0, hot_count - 1)
    hot_rows = jnp.take_along_axis(hot_all, hot_pick[:, :, None], axis=1).reshape(count, lsize)
    merged = jnp.where(is_cold[:, None], cold_rows, hot_rows).reshape(qcount, nprobe * lsize)
    return lax.top_k(merged, TOPK)[0]


def batcher(n):
    pairs = []
    p = 1
    while p < n:
        k = p
        while k >= 1:
            for j in range(k % p, n - k, 2 * k):
                for i in range(min(k, n - j - k)):
                    if (i + j) // (2 * p) == (i + j + k) // (2 * p):
                        pairs.append((i + j, i + j + k))
            k //= 2
        p *= 2
    return pairs


def exchange(vals, a, b):
    x, y = vals[a], vals[b]
    vals[a], vals[b] = jnp.maximum(x, y), jnp.minimum(x, y)


def clean(vals, where, dists):
    for d in dists:
        for i in range(len(where)):
            if i & d == 0:
                exchange(vals, where[i], where[i + d])


def at(i):
    return pl.ds(pl.multiple_of(i * SUB, SUB), SUB)


def loop(n, unroll, body):
    @pl.loop(0, n // unroll)
    def _(step):
        for u in range(unroll):
            body(step * unroll + u)


def sort_runs(ref, count):
    net = batcher(32)

    def body(t):
        vals = [ref[at(t * 32 + i), :] for i in range(32)]
        for a, b in net:
            exchange(vals, a, b)
        for i in range(32):
            ref[at(t * 32 + i), :] = vals[i]

    loop(count // 32, 1, body)


def join_runs(ref, count, half):
    size = 2 * half
    step = half // 4
    per = 4

    @pl.loop(0, count // size * step // per)
    def _(t):
        base = t * per // step * size
        first = t * per % step
        work = []
        for u in range(per):
            i = first + u
            idx = [base + i + step * k for k in range(4)]
            idx += [base + size - 1 - i - step * k for k in range(4)]
            work.append((idx, [ref[at(x), :] for x in idx]))
        for _, vals in work:
            for k in range(4):
                exchange(vals, k, 4 + k)
            clean(vals, [0, 1, 2, 3], (2, 1))
            clean(vals, [7, 6, 5, 4], (2, 1))
        for idx, vals in work:
            for x, v in zip(idx, vals):
                ref[at(x), :] = v

    tidy(ref, ref, count, step)


def tidy(src, dst, count, block):
    dists = []
    d = block // 2
    while d:
        dists.append(d)
        d //= 2

    @pl.loop(0, count // 32)
    def _(t):
        vals = [src[at(t * 32 + i), :] for i in range(32)]
        for c in range(32 // block):
            clean(vals, list(range(c * block, (c + 1) * block)), dists)
        for i in range(32):
            dst[at(t * 32 + i), :] = vals[i]


def best_of(a, abase, b, bbase, tmp, dst, turn=0):
    step = TOPK // 8
    per = 2

    @pl.loop(0, step // per)
    def _(t):
        work = []
        for u in range(per):
            i = t * per + u
            vals = []
            for k in range(8):
                x = a[at(abase + i + step * k), :]
                y = b[at(bbase + TOPK - 1 - i - step * k), :]
                if turn:
                    y = pltpu.roll(y, turn, 0)
                vals.append(jnp.maximum(x, y))
            work.append(vals)
        for vals in work:
            clean(vals, list(range(8)), (4, 2, 1))
        for u, vals in enumerate(work):
            for k in range(8):
                tmp[at(t * per + u + step * k), :] = vals[k]

    tidy(tmp, dst, TOPK, step)


def fused(
    rows, cap, q_ref, hot_ref, cold_ref, out_ref,
    q_all, key, onehot, work, short, tmp, runs, hotbest, keep, pairbuf, sendbuf, mergebuf, recv,
    gs_sem, gr_sem, ps_sem, pr_sem, ss_sem, sr_sem,
):
    me = lax.axis_index("row")
    core = lax.rem(me, 2)
    partner = me + 1 - 2 * core
    across = me + 2 - 4 * lax.rem(me // 2, 2)
    hot_count, lsize = hot_ref.shape[0], hot_ref.shape[1]
    qcount = LANES
    nprobe = q_ref.shape[0] - qcount
    list_dev = cold_ref.shape[0]
    pack = LANES // cap
    groups = rows // pack
    f32 = jnp.float32

    def remote(src, dst, send_sem, recv_sem, to):
        return pltpu.make_async_remote_copy(
            src_ref=src, dst_ref=dst, send_sem=send_sem, recv_sem=recv_sem,
            device_id={"row": to}, device_id_type=pl.DeviceIdType.MESH,
        )

    def gather_copy(source, kind, step, to):
        src = q_ref if step == 0 and kind != 2 else q_all.at[source]
        return remote(src, q_all.at[source], gs_sem.at[kind, step], gr_sem.at[source], to)

    def line(step):
        return lax.rem(me + pack * step, rows)

    def column(step):
        return lax.rem(across + pack * step, rows)

    def arrived(source):
        gather_copy(source, 2, 0, partner).wait_recv()

    def relay_line(step):
        if step:
            arrived(line(step))
        gather_copy(line(step), 0, step, across).start()
        gather_copy(line(step), 1, step, partner).start()

    def relay_column(step):
        arrived(column(step))
        gather_copy(column(step), 2, step, partner).start()

    def pair_copy(step, k):
        return remote(
            sendbuf.at[step, 2 * k + 1 - core], pairbuf.at[step, k],
            ps_sem.at[step, k], pr_sem.at[step, k], partner,
        )

    def final_copy(step, k, to, source):
        return remote(
            mergebuf.at[step, 2 * k + core], recv.at[source], ss_sem.at[step, k], sr_sem.at[source], to
        )

    barrier = pltpu.get_barrier_semaphore()

    @pl.loop(1, rows)
    def _(d):
        pl.semaphore_signal(
            barrier, inc=1, device_id={"row": lax.rem(me + d, rows)},
            device_id_type=pl.DeviceIdType.MESH,
        )

    pl.semaphore_wait(barrier, rows - 1)

    relay_line(0)
    for step in range(1, groups):
        remote(
            q_ref, q_all.at[me], gs_sem.at[3, step], gr_sem.at[me], lax.rem(me + rows - pack * step, rows)
        ).start()
    q_all[me] = q_ref[...]

    before = (
        lax.broadcasted_iota(jnp.int32, (qcount, qcount), 0)
        < lax.broadcasted_iota(jnp.int32, (qcount, qcount), 1)
    )
    before = jnp.where(before, 1.0, 0.0).astype(jnp.bfloat16)

    def keys_of(pt, first, count):
        ids = (first + lax.broadcasted_iota(jnp.int32, (count, qcount), 0)).astype(f32)
        pt = pt.astype(f32)
        named = pt[0:1, :] == ids
        for j in range(1, nprobe):
            named = named | (pt[j : j + 1, :] == ids)
        ones = jnp.where(named, 1.0, 0.0)
        rank = jnp.dot(ones.astype(jnp.bfloat16), before, preferred_element_type=f32)
        return named, rank

    slot_row = lax.broadcasted_iota(jnp.int32, (LANES, pack * qcount), 0).astype(f32)
    lane = lax.broadcasted_iota(jnp.int32, (lsize, LANES), 1)

    def match(l):
        hit = slot_row == key[l : l + 1, :]
        hot1 = jnp.where(hit, 1.0, 0.0).astype(jnp.bfloat16)
        onehot[l] = hot1
        return hot1

    def spread(l, half):
        part = short[pl.ds(l, TOPK, stride=SUB), :]
        high = part.astype(jnp.bfloat16)
        low = (part - high.astype(f32)).astype(jnp.bfloat16)
        hot1 = onehot[l]
        full = jnp.dot(high, hot1, preferred_element_type=f32)
        full = full + jnp.dot(low, hot1, preferred_element_type=f32)
        full = jnp.where(key[l : l + 1, :] >= 0.0, full, LOW)
        for b in range(pack):
            runs[l // half, pl.ds((l % half) * pack + b, TOPK, stride=SUB), :] = full[
                :, b * qcount : (b + 1) * qcount
            ]

    def shorten():
        sort_runs(work, lsize)
        join_runs(work, lsize, 32)
        join_runs(work, lsize, 64)
        best_of(work, 0, work, TOPK, tmp, short)

    half = SUB // pack

    named, rank = keys_of(q_ref[qcount : qcount + nprobe, :qcount], 0, hot_count)
    for l in range(hot_count):
        value = jnp.where(named[l : l + 1, :], rank[l : l + 1, :] + float(cap * (l % pack)), -1.0)
        key[l // pack : l // pack + 1, (l % pack) * qcount : (l % pack + 1) * qcount] = value
    mine = q_ref[:qcount, :]
    stack = jnp.concatenate([mine] * pack, axis=0)
    for t in range(hot_count // pack):
        rows_t = jnp.dot(match(t), stack, preferred_element_type=f32).astype(jnp.bfloat16)
        score = None
        for c in range(pack):
            one = lax.dot_general(
                hot_ref[t * pack + c], rows_t, (((1,), (1,)), ((), ())), preferred_element_type=f32
            )
            score = one if score is None else jnp.where(lane >= c * cap, one, score)
        work[pl.ds(t, lsize, stride=SUB), :] = score
        work[pl.ds(hot_count // pack + t, lsize, stride=SUB), :] = score
    relay_column(0)
    shorten()
    relay_line(1)
    for t in range(hot_count // pack):
        spread(t, half)
    best_of(runs.at[0], 0, runs.at[1], 0, tmp, hotbest)
    relay_line(2)
    relay_column(1)

    def merge_out(step):
        g = lax.rem(me // pack + step, groups)
        for k in range(pack // 2):
            pair_copy(step, k).wait_recv()
            part = pairbuf[step, k]
            for c in range(2):
                runs[3, pl.ds(2 * k + c, TOPK, stride=SUB), :] = part
        best_of(keep.at[step], 0, runs.at[3], 0, tmp, runs.at[2])
        for b in range(pack):
            mergebuf[step, b] = runs[2, pl.ds(b, TOPK, stride=SUB), :]
        for k in range(pack // 2):
            to = g * pack + 2 * k + core

            @pl.when(to != me)
            def _():
                final_copy(step, k, to, me // 2).start()

            @pl.when(to == me)
            def _():
                recv[me // 2] = mergebuf[step, 2 * k + core]

    @pl.loop(0, groups)
    def _(step):
        g = lax.rem(me // pack + step, groups)
        arrived(lax.rem(partner + pack * step, rows))
        arrived(lax.rem(across + partner - me + pack * step, rows))
        for b in range(pack):
            block = g * pack + b
            named, rank = keys_of(
                q_all[block, qcount : qcount + nprobe, :qcount], hot_count + me * list_dev, list_dev
            )
            key[:, b * qcount : (b + 1) * qcount] = jnp.where(named, rank + float(cap * b), -1.0)
        stack = jnp.concatenate([q_all[g * pack + b, :qcount, :] for b in range(pack)], axis=0)
        for l in range(list_dev):
            rows_l = jnp.dot(match(l), stack, preferred_element_type=f32).astype(jnp.bfloat16)
            work[pl.ds(l, lsize, stride=SUB), :] = lax.dot_general(
                cold_ref[l], rows_l, (((1,), (1,)), ((), ())), preferred_element_type=f32
            )

        @pl.when(step == 0)
        def _():
            relay_line(3)
            relay_column(2)

        shorten()

        @pl.when(step == 0)
        def _():
            relay_column(3)

        @pl.when(step >= 1)
        def _():
            merge_out(step - 1)

        for l in range(list_dev):
            spread(l, half)
        best_of(runs.at[0], 0, runs.at[1], 0, tmp, runs.at[0])
        best_of(runs.at[2], 0, runs.at[3], 0, tmp, runs.at[2])
        best_of(runs.at[0], 0, runs.at[2], 0, tmp, runs.at[0])
        best_of(runs.at[0], 0, runs.at[0], 0, tmp, keep.at[step], turn=pack)
        for b in range(pack):
            sendbuf[step, b] = keep[step, pl.ds(b, TOPK, stride=SUB), :]
        for k in range(pack // 2):
            pair_copy(step, k).start()

    merge_out(groups - 1)

    @pl.loop(1, rows // 2)
    def _(d):
        source = lax.rem(me // 2 + d, rows // 2)
        final_copy(0, 0, partner, source).wait_recv()

    for o in range(rows // 2):
        runs[0, pl.ds(o, TOPK, stride=SUB), :] = recv[o]
    best_of(hotbest, 0, runs.at[0], 0, tmp, hotbest)
    turn = SUB // 2
    src, dst = hotbest, runs.at[0]
    while turn:
        best_of(src, 0, src, 0, tmp, dst, turn=turn)
        src, dst = dst, src
        turn //= 2
    result = src[pl.ds(0, TOPK, stride=SUB), :]
    out_ref[...] = result.T

    for step in range(groups):
        gather_copy(line(step), 0, step, across).wait_send()
        gather_copy(line(step), 1, step, partner).wait_send()
        gather_copy(column(step), 2, step, partner).wait_send()
        if step:
            remote(q_ref, q_all.at[me], gs_sem.at[3, step], gr_sem.at[me], partner).wait_send()
        for k in range(pack // 2):
            pair_copy(step, k).wait_send()
            to = lax.rem(me // pack + step, groups) * pack + 2 * k + core

            @pl.when(to != me)
            def _():
                final_copy(step, k, to, me // 2).wait_send()


def shards(queries, probes, hot_lists, cold_lists):
    rows = lax.axis_size("row")
    qcount, nprobe = probes.shape
    list_dev = cold_lists.shape[0]
    hot_count, lsize, width = hot_lists.shape
    cap = 2 * ((qcount * nprobe + list_dev * rows - 1) // (list_dev * rows))
    pack = LANES // cap
    fits = (
        qcount == LANES and lsize == 2 * TOPK and list_dev == SUB and pack == 4
        and hot_count == pack * pack and rows == 2 * SUB and width >= qcount
        and hot_count + list_dev * rows <= 256
    )
    if not fits:
        return general(queries, probes, hot_lists, cold_lists)
    vmem = pl.BlockSpec(memory_space=pltpu.VMEM)
    dma = pltpu.SemaphoreType.DMA
    groups = rows // pack
    ids = jnp.pad(probes.T, ((0, 0), (0, width - qcount))).astype(jnp.bfloat16)
    held = jnp.concatenate([queries, ids], axis=0)
    run = pltpu.VMEM((TOPK * SUB, LANES), jnp.float32)
    return pl.pallas_call(
        functools.partial(fused, rows, cap),
        out_shape=jax.ShapeDtypeStruct((qcount, TOPK), jnp.float32),
        in_specs=[vmem] * 3,
        out_specs=vmem,
        scratch_shapes=[
            pltpu.VMEM((rows,) + held.shape, jnp.bfloat16),
            pltpu.VMEM((list_dev, pack * qcount), jnp.float32),
            pltpu.VMEM((list_dev, LANES, pack * qcount), jnp.bfloat16),
            pltpu.VMEM((lsize * SUB, LANES), jnp.float32),
            run,
            run,
            pltpu.VMEM((list_dev * pack // SUB, TOPK * SUB, LANES), jnp.float32),
            run,
            pltpu.VMEM((groups, TOPK * SUB, LANES), jnp.float32),
            pltpu.VMEM((groups, pack // 2, TOPK, qcount), jnp.float32),
            pltpu.VMEM((groups, pack, TOPK, qcount), jnp.float32),
            pltpu.VMEM((groups, pack, TOPK, qcount), jnp.float32),
            pltpu.VMEM((rows // 2, TOPK, qcount), jnp.float32),
            dma((4, groups)),
            dma((rows,)),
            dma((groups, pack // 2)),
            dma((groups, pack // 2)),
            dma((groups, pack // 2)),
            dma((rows // 2,)),
        ],
        compiler_params=pltpu.CompilerParams(
            collective_id=0, has_side_effects=True, vmem_limit_bytes=48 * 1024 * 1024
        ),
    )(held, hot_lists, cold_lists)


def solution(mesh):
    placed = (
        P(("tenant", "row"), None),
        P(("tenant", "row"), None),
        P("tenant", None, None),
        P(("tenant", "row"), None, None),
    )
    return jax.shard_map(
        shards, mesh=mesh, in_specs=placed, out_specs=P(("tenant", "row"), None), check_vma=False
    )
```

```python
import functools
import math

import jax
import jax.numpy as jnp
from jax import lax
from jax.experimental import pallas as pl
from jax.experimental.pallas import tpu as pltpu
from jax.sharding import PartitionSpec as P

TOPK = 128
LOW = -3.0e38
SUB = 8
LANES = 128


def hot_scores(queries, hot_lists):
    hot_count, lsize, width = hot_lists.shape
    qcount = queries.shape[0]
    flat_hot = hot_lists.reshape(hot_count * lsize, width)
    scores = lax.dot_general(
        queries, flat_hot, (((1,), (1,)), ((), ())), preferred_element_type=jnp.float32
    )
    return scores.reshape(qcount, hot_count, lsize)


def earlier_equal(flat):
    count = flat.shape[0]
    block = math.gcd(count, 512)
    index_all = jnp.arange(count, dtype=jnp.int32)

    def one_block(start):
        ids = lax.dynamic_slice_in_dim(flat, start, block, 0)
        where_at = start + jnp.arange(block, dtype=jnp.int32)
        same = (ids[:, None] == flat[None, :]) & (index_all[None, :] < where_at[:, None])
        return jnp.sum(same.astype(jnp.int32), axis=1)

    starts = jnp.arange(count // block, dtype=jnp.int32) * block
    return lax.map(one_block, starts).reshape(count)


def general(queries, probes, hot_lists, cold_lists):
    rows = lax.axis_size("row")
    qcount, nprobe = probes.shape
    list_dev = cold_lists.shape[0]
    hot_count, lsize, width = hot_lists.shape
    capacity = 2 * ((qcount * nprobe + list_dev * rows - 1) // (list_dev * rows))
    total = rows * list_dev * capacity
    flat = probes.reshape(-1)
    count = flat.shape[0]
    pair_query = jnp.arange(count, dtype=jnp.int32) // nprobe
    rank = earlier_equal(flat)
    cold_id = flat - hot_count
    is_cold = cold_id >= 0
    slot = jnp.where(is_cold, cold_id * capacity + rank, total)
    outgoing = (
        jnp.zeros((total, width), jnp.bfloat16).at[slot].set(queries[pair_query], mode="drop")
    )
    outgoing = outgoing.reshape(rows, list_dev, capacity, width)
    arrived = lax.all_to_all(outgoing, "row", split_axis=0, concat_axis=0, tiled=True)
    scores = jnp.einsum("slcd,lvd->slcv", arrived, cold_lists, preferred_element_type=jnp.float32)
    reading = jnp.minimum(slot, total - 1)
    returned = lax.all_to_all(scores, "row", split_axis=0, concat_axis=0, tiled=True).reshape(
        total, lsize
    )
    cold_rows = returned[reading]
    hot_all = hot_scores(queries, hot_lists)
    hot_pick = jnp.clip(probes, 0, hot_count - 1)
    hot_rows = jnp.take_along_axis(hot_all, hot_pick[:, :, None], axis=1).reshape(count, lsize)
    merged = jnp.where(is_cold[:, None], cold_rows, hot_rows).reshape(qcount, nprobe * lsize)
    return lax.top_k(merged, TOPK)[0]


def batcher(n):
    pairs = []
    p = 1
    while p < n:
        k = p
        while k >= 1:
            for j in range(k % p, n - k, 2 * k):
                for i in range(min(k, n - j - k)):
                    if (i + j) // (2 * p) == (i + j + k) // (2 * p):
                        pairs.append((i + j, i + j + k))
            k //= 2
        p *= 2
    return pairs


def exchange(vals, a, b):
    x, y = vals[a], vals[b]
    vals[a], vals[b] = jnp.maximum(x, y), jnp.minimum(x, y)


def clean(vals, where, dists):
    for d in dists:
        for i in range(len(where)):
            if i & d == 0:
                exchange(vals, where[i], where[i + d])


def at(i):
    return pl.ds(i * SUB, SUB)


def sort_runs(ref, count):
    net = batcher(32)

    @pl.loop(0, count // 32)
    def _(t):
        start = pl.multiple_of(t * (32 * SUB), 32 * SUB)
        vals = [ref[pl.ds(start + i * SUB, SUB), :] for i in range(32)]
        for a, b in net:
            exchange(vals, a, b)
        for i in range(32):
            ref[pl.ds(start + i * SUB, SUB), :] = vals[i]


def join_runs(ref, count, half):
    size = 2 * half
    step = half // 4
    for base in range(0, count, size):
        for i in range(base, base + step):
            idx = [i + step * k for k in range(4)]
            idx += [2 * base + size - 1 - x for x in idx]
            vals = [ref[at(x), :] for x in idx]
            for k in range(4):
                exchange(vals, k, 4 + k)
            clean(vals, [0, 1, 2, 3], (2, 1))
            clean(vals, [7, 6, 5, 4], (2, 1))
            for x, v in zip(idx, vals):
                ref[at(x), :] = v
    tidy(ref, ref, count, step)


def tidy(src, dst, count, block):
    dists = []
    d = block // 2
    while d:
        dists.append(d)
        d //= 2
    for start in range(0, count, block):
        vals = [src[at(start + i), :] for i in range(block)]
        clean(vals, list(range(block)), dists)
        for i in range(block):
            dst[at(start + i), :] = vals[i]


def best_of(a, abase, b, bbase, tmp, dst, turn=0):
    step = TOPK // 8
    for i in range(step):
        vals = []
        for k in range(8):
            x = a[at(abase + i + step * k), :]
            y = b[at(bbase + TOPK - 1 - i - step * k), :]
            if turn:
                y = pltpu.roll(y, turn, 0)
            vals.append(jnp.maximum(x, y))
        clean(vals, list(range(8)), (4, 2, 1))
        for k in range(8):
            tmp[at(i + step * k), :] = vals[k]
    tidy(tmp, dst, TOPK, step)


def fused(
    rows, cap, q_ref, hot_hbm, cold_hbm, out_ref,
    hot_ref, cold_ref, list_sem, q_all, key, onehot, work, short, tmp, runs, hotbest, keep, pairbuf, sendbuf, mergebuf, recv,
    gs_sem, gr_sem, ps_sem, pr_sem, ss_sem, sr_sem,
):
    fetch_hot = pltpu.make_async_copy(hot_hbm, hot_ref, list_sem.at[0])
    fetch_cold = pltpu.make_async_copy(cold_hbm, cold_ref, list_sem.at[1])
    fetch_hot.start()
    fetch_cold.start()
    me = lax.axis_index("row")
    core = lax.rem(me, 2)
    partner = me + 1 - 2 * core
    across = me + 2 - 4 * lax.rem(me // 2, 2)
    hot_count, lsize = hot_ref.shape[0], hot_ref.shape[1]
    qcount = LANES
    nprobe = q_ref.shape[0] - qcount
    list_dev = cold_ref.shape[0]
    pack = LANES // cap
    groups = rows // pack
    f32 = jnp.float32

    def remote(src, dst, send_sem, recv_sem, to):
        return pltpu.make_async_remote_copy(
            src_ref=src, dst_ref=dst, send_sem=send_sem, recv_sem=recv_sem,
            device_id={"row": to}, device_id_type=pl.DeviceIdType.MESH,
        )

    def gather_copy(source, kind, step, to):
        src = q_ref if step == 0 and kind != 2 else q_all.at[source]
        return remote(src, q_all.at[source], gs_sem.at[kind, step], gr_sem.at[source], to)

    def line(step):
        return lax.rem(me + pack * step, rows)

    def column(step):
        return lax.rem(across + pack * step, rows)

    def arrived(source):
        gather_copy(source, 2, 0, partner).wait_recv()

    def relay_line(step):
        if step:
            arrived(line(step))
        gather_copy(line(step), 0, step, across).start()
        gather_copy(line(step), 1, step, partner).start()

    def relay_column(step):
        arrived(column(step))
        gather_copy(column(step), 2, step, partner).start()

    def pair_copy(step, k):
        return remote(
            sendbuf.at[step, 2 * k + 1 - core], pairbuf.at[step, k],
            ps_sem.at[step, k], pr_sem.at[step, k], partner,
        )

    def final_copy(step, k, to, source):
        return remote(
            mergebuf.at[step, 2 * k + core], recv.at[source], ss_sem.at[step, k], sr_sem.at[source], to
        )

    barrier = pltpu.get_barrier_semaphore()

    @pl.loop(1, rows)
    def _(d):
        pl.semaphore_signal(
            barrier, inc=1, device_id={"row": lax.rem(me + d, rows)},
            device_id_type=pl.DeviceIdType.MESH,
        )

    pl.semaphore_wait(barrier, rows - 1)

    relay_line(0)
    for step in range(1, groups):
        remote(
            q_ref, q_all.at[me], gs_sem.at[3, step], gr_sem.at[me], lax.rem(me + rows - pack * step, rows)
        ).start()
    q_all[me] = q_ref[...]

    before = (
        lax.broadcasted_iota(jnp.int32, (qcount, qcount), 0)
        < lax.broadcasted_iota(jnp.int32, (qcount, qcount), 1)
    )
    before = jnp.where(before, 1.0, 0.0).astype(jnp.bfloat16)

    def keys_of(pt, first, count):
        ids = (first + lax.broadcasted_iota(jnp.int32, (count, qcount), 0)).astype(f32)
        pt = pt.astype(f32)
        named = pt[0:1, :] == ids
        for j in range(1, nprobe):
            named = named | (pt[j : j + 1, :] == ids)
        ones = jnp.where(named, 1.0, 0.0)
        rank = jnp.dot(ones.astype(jnp.bfloat16), before, preferred_element_type=f32)
        return named, rank

    slot_row = lax.broadcasted_iota(jnp.int32, (LANES, pack * qcount), 0).astype(f32)
    lane = lax.broadcasted_iota(jnp.int32, (lsize, LANES), 1)

    def match(l):
        hit = slot_row == key[l : l + 1, :]
        hot1 = jnp.where(hit, 1.0, 0.0).astype(jnp.bfloat16)
        onehot[l] = hot1
        return hot1

    def spread(l, half):
        part = short[pl.ds(l, TOPK, stride=SUB), :]
        high = part.astype(jnp.bfloat16)
        low = (part - high.astype(f32)).astype(jnp.bfloat16)
        hot1 = onehot[l]
        full = jnp.dot(high, hot1, preferred_element_type=f32)
        full = full + jnp.dot(low, hot1, preferred_element_type=f32)
        full = jnp.where(key[l : l + 1, :] >= 0.0, full, LOW)
        for b in range(pack):
            runs[l // half, pl.ds((l % half) * pack + b, TOPK, stride=SUB), :] = full[
                :, b * qcount : (b + 1) * qcount
            ]

    def shorten():
        sort_runs(work, lsize)
        join_runs(work, lsize, 32)
        join_runs(work, lsize, 64)
        best_of(work, 0, work, TOPK, tmp, short)

    half = SUB // pack

    named, rank = keys_of(q_ref[qcount : qcount + nprobe, :qcount], 0, hot_count)
    for l in range(hot_count):
        value = jnp.where(named[l : l + 1, :], rank[l : l + 1, :] + float(cap * (l % pack)), -1.0)
        key[l // pack : l // pack + 1, (l % pack) * qcount : (l % pack + 1) * qcount] = value
    mine = q_ref[:qcount, :]
    stack = jnp.concatenate([mine] * pack, axis=0)
    fetch_hot.wait()
    for t in range(hot_count // pack):
        rows_t = jnp.dot(match(t), stack, preferred_element_type=f32).astype(jnp.bfloat16)
        score = None
        for c in range(pack):
            one = lax.dot_general(
                hot_ref[t * pack + c], rows_t, (((1,), (1,)), ((), ())), preferred_element_type=f32
            )
            score = one if score is None else jnp.where(lane >= c * cap, one, score)
        work[pl.ds(t, lsize, stride=SUB), :] = score
        work[pl.ds(hot_count // pack + t, lsize, stride=SUB), :] = score
    relay_column(0)
    shorten()
    relay_line(1)
    for t in range(hot_count // pack):
        spread(t, half)
    best_of(runs.at[0], 0, runs.at[1], 0, tmp, hotbest)
    relay_line(2)
    relay_column(1)
    fetch_cold.wait()

    def merge_out(step):
        g = lax.rem(me // pack + step, groups)
        for k in range(pack // 2):
            pair_copy(step, k).wait_recv()
            part = pairbuf[step, k]
            for c in range(2):
                runs[3, pl.ds(2 * k + c, TOPK, stride=SUB), :] = part
        best_of(keep.at[step], 0, runs.at[3], 0, tmp, runs.at[2])
        for b in range(pack):
            mergebuf[step, b] = runs[2, pl.ds(b, TOPK, stride=SUB), :]
        for k in range(pack // 2):
            to = g * pack + 2 * k + core

            @pl.when(to != me)
            def _():
                final_copy(step, k, to, me // 2).start()

            @pl.when(to == me)
            def _():
                recv[me // 2] = mergebuf[step, 2 * k + core]

    @pl.loop(0, groups)
    def _(step):
        g = lax.rem(me // pack + step, groups)
        arrived(lax.rem(partner + pack * step, rows))
        arrived(lax.rem(across + partner - me + pack * step, rows))
        for b in range(pack):
            block = g * pack + b
            named, rank = keys_of(
                q_all[block, qcount : qcount + nprobe, :qcount], hot_count + me * list_dev, list_dev
            )
            key[:, b * qcount : (b + 1) * qcount] = jnp.where(named, rank + float(cap * b), -1.0)
        stack = jnp.concatenate([q_all[g * pack + b, :qcount, :] for b in range(pack)], axis=0)
        for l in range(list_dev):
            rows_l = jnp.dot(match(l), stack, preferred_element_type=f32).astype(jnp.bfloat16)
            work[pl.ds(l, lsize, stride=SUB), :] = lax.dot_general(
                cold_ref[l], rows_l, (((1,), (1,)), ((), ())), preferred_element_type=f32
            )

        @pl.when(step == 0)
        def _():
            relay_line(3)
            relay_column(2)

        shorten()

        @pl.when(step == 0)
        def _():
            relay_column(3)

        @pl.when(step >= 1)
        def _():
            merge_out(step - 1)

        for l in range(list_dev):
            spread(l, half)
        best_of(runs.at[0], 0, runs.at[1], 0, tmp, runs.at[0])
        best_of(runs.at[2], 0, runs.at[3], 0, tmp, runs.at[2])
        best_of(runs.at[0], 0, runs.at[2], 0, tmp, runs.at[0])
        best_of(runs.at[0], 0, runs.at[0], 0, tmp, keep.at[step], turn=pack)
        for b in range(pack):
            sendbuf[step, b] = keep[step, pl.ds(b, TOPK, stride=SUB), :]
        for k in range(pack // 2):
            pair_copy(step, k).start()

    merge_out(groups - 1)

    @pl.loop(1, rows // 2)
    def _(d):
        source = lax.rem(me // 2 + d, rows // 2)
        final_copy(0, 0, partner, source).wait_recv()

    for o in range(rows // 2):
        runs[0, pl.ds(o, TOPK, stride=SUB), :] = recv[o]
    best_of(hotbest, 0, runs.at[0], 0, tmp, hotbest)
    turn = SUB // 2
    src, dst = hotbest, runs.at[0]
    while turn:
        best_of(src, 0, src, 0, tmp, dst, turn=turn)
        src, dst = dst, src
        turn //= 2
    result = src[pl.ds(0, TOPK, stride=SUB), :]
    out_ref[...] = result.T

    for step in range(groups):
        gather_copy(line(step), 0, step, across).wait_send()
        gather_copy(line(step), 1, step, partner).wait_send()
        gather_copy(column(step), 2, step, partner).wait_send()
        if step:
            remote(q_ref, q_all.at[me], gs_sem.at[3, step], gr_sem.at[me], partner).wait_send()
        for k in range(pack // 2):
            pair_copy(step, k).wait_send()
            to = lax.rem(me // pack + step, groups) * pack + 2 * k + core

            @pl.when(to != me)
            def _():
                final_copy(step, k, to, me // 2).wait_send()


def shards(queries, probes, hot_lists, cold_lists):
    rows = lax.axis_size("row")
    qcount, nprobe = probes.shape
    list_dev = cold_lists.shape[0]
    hot_count, lsize, width = hot_lists.shape
    cap = 2 * ((qcount * nprobe + list_dev * rows - 1) // (list_dev * rows))
    pack = LANES // cap
    fits = (
        qcount == LANES and lsize == 2 * TOPK and list_dev == SUB and pack == 4
        and hot_count == pack * pack and rows == 2 * SUB and width >= qcount
        and hot_count + list_dev * rows <= 256
    )
    if not fits:
        return general(queries, probes, hot_lists, cold_lists)
    vmem = pl.BlockSpec(memory_space=pltpu.VMEM)
    far = pl.BlockSpec(memory_space=pl.ANY)
    dma = pltpu.SemaphoreType.DMA
    groups = rows // pack
    ids = jnp.pad(probes.T, ((0, 0), (0, width - qcount))).astype(jnp.bfloat16)
    held = jnp.concatenate([queries, ids], axis=0)
    run = pltpu.VMEM((TOPK * SUB, LANES), jnp.float32)
    return pl.pallas_call(
        functools.partial(fused, rows, cap),
        out_shape=jax.ShapeDtypeStruct((qcount, TOPK), jnp.float32),
        in_specs=[vmem, far, far],
        out_specs=vmem,
        scratch_shapes=[
            pltpu.VMEM(hot_lists.shape, jnp.bfloat16),
            pltpu.VMEM(cold_lists.shape, jnp.bfloat16),
            dma((2,)),
            pltpu.VMEM((rows,) + held.shape, jnp.bfloat16),
            pltpu.VMEM((list_dev, pack * qcount), jnp.float32),
            pltpu.VMEM((list_dev, LANES, pack * qcount), jnp.bfloat16),
            pltpu.VMEM((lsize * SUB, LANES), jnp.float32),
            run,
            run,
            pltpu.VMEM((list_dev * pack // SUB, TOPK * SUB, LANES), jnp.float32),
            run,
            pltpu.VMEM((groups, TOPK * SUB, LANES), jnp.float32),
            pltpu.VMEM((groups, pack // 2, TOPK, qcount), jnp.float32),
            pltpu.VMEM((groups, pack, TOPK, qcount), jnp.float32),
            pltpu.VMEM((groups, pack, TOPK, qcount), jnp.float32),
            pltpu.VMEM((rows // 2, TOPK, qcount), jnp.float32),
            dma((4, groups)),
            dma((rows,)),
            dma((groups, pack // 2)),
            dma((groups, pack // 2)),
            dma((groups, pack // 2)),
            dma((rows // 2,)),
        ],
        compiler_params=pltpu.CompilerParams(
            collective_id=0, has_side_effects=True, vmem_limit_bytes=60 * 1024 * 1024
        ),
    )(held, hot_lists, cold_lists)


def solution(mesh):
    placed = (
        P(("tenant", "row"), None),
        P(("tenant", "row"), None),
        P("tenant", None, None),
        P(("tenant", "row"), None, None),
    )
    return jax.shard_map(
        shards, mesh=mesh, in_specs=placed, out_specs=P(("tenant", "row"), None), check_vma=False
    )
```

```python
import functools
import math

import jax
import jax.numpy as jnp
from jax import lax
from jax.experimental import pallas as pl
from jax.experimental.pallas import tpu as pltpu
from jax.sharding import PartitionSpec as P

TOPK = 128
LOW = -3.0e38
SUB = 8
LANES = 128


def hot_scores(queries, hot_lists):
    hot_count, lsize, width = hot_lists.shape
    qcount = queries.shape[0]
    flat_hot = hot_lists.reshape(hot_count * lsize, width)
    scores = lax.dot_general(
        queries, flat_hot, (((1,), (1,)), ((), ())), preferred_element_type=jnp.float32
    )
    return scores.reshape(qcount, hot_count, lsize)


def earlier_equal(flat):
    count = flat.shape[0]
    block = math.gcd(count, 512)
    index_all = jnp.arange(count, dtype=jnp.int32)

    def one_block(start):
        ids = lax.dynamic_slice_in_dim(flat, start, block, 0)
        where_at = start + jnp.arange(block, dtype=jnp.int32)
        same = (ids[:, None] == flat[None, :]) & (index_all[None, :] < where_at[:, None])
        return jnp.sum(same.astype(jnp.int32), axis=1)

    starts = jnp.arange(count // block, dtype=jnp.int32) * block
    return lax.map(one_block, starts).reshape(count)


def general(queries, probes, hot_lists, cold_lists):
    rows = lax.axis_size("row")
    qcount, nprobe = probes.shape
    list_dev = cold_lists.shape[0]
    hot_count, lsize, width = hot_lists.shape
    capacity = 2 * ((qcount * nprobe + list_dev * rows - 1) // (list_dev * rows))
    total = rows * list_dev * capacity
    flat = probes.reshape(-1)
    count = flat.shape[0]
    pair_query = jnp.arange(count, dtype=jnp.int32) // nprobe
    rank = earlier_equal(flat)
    cold_id = flat - hot_count
    is_cold = cold_id >= 0
    slot = jnp.where(is_cold, cold_id * capacity + rank, total)
    outgoing = (
        jnp.zeros((total, width), jnp.bfloat16).at[slot].set(queries[pair_query], mode="drop")
    )
    outgoing = outgoing.reshape(rows, list_dev, capacity, width)
    arrived = lax.all_to_all(outgoing, "row", split_axis=0, concat_axis=0, tiled=True)
    scores = jnp.einsum("slcd,lvd->slcv", arrived, cold_lists, preferred_element_type=jnp.float32)
    reading = jnp.minimum(slot, total - 1)
    returned = lax.all_to_all(scores, "row", split_axis=0, concat_axis=0, tiled=True).reshape(
        total, lsize
    )
    cold_rows = returned[reading]
    hot_all = hot_scores(queries, hot_lists)
    hot_pick = jnp.clip(probes, 0, hot_count - 1)
    hot_rows = jnp.take_along_axis(hot_all, hot_pick[:, :, None], axis=1).reshape(count, lsize)
    merged = jnp.where(is_cold[:, None], cold_rows, hot_rows).reshape(qcount, nprobe * lsize)
    return lax.top_k(merged, TOPK)[0]


def batcher(n):
    pairs = []
    p = 1
    while p < n:
        k = p
        while k >= 1:
            for j in range(k % p, n - k, 2 * k):
                for i in range(min(k, n - j - k)):
                    if (i + j) // (2 * p) == (i + j + k) // (2 * p):
                        pairs.append((i + j, i + j + k))
            k //= 2
        p *= 2
    return pairs


def exchange(vals, a, b):
    x, y = vals[a], vals[b]
    vals[a], vals[b] = jnp.maximum(x, y), jnp.minimum(x, y)


def clean(vals, where, dists):
    for d in dists:
        for i in range(len(where)):
            if i & d == 0:
                exchange(vals, where[i], where[i + d])


def at(i):
    return pl.ds(i * SUB, SUB)


def sort_runs(ref, count):
    net = batcher(32)

    @pl.loop(0, count // 32)
    def _(t):
        start = pl.multiple_of(t * (32 * SUB), 32 * SUB)
        vals = [ref[pl.ds(start + i * SUB, SUB), :] for i in range(32)]
        for a, b in net:
            exchange(vals, a, b)
        for i in range(32):
            ref[pl.ds(start + i * SUB, SUB), :] = vals[i]


def join_runs(ref, count, half):
    size = 2 * half
    step = half // 4
    for base in range(0, count, size):
        for i in range(base, base + step):
            idx = [i + step * k for k in range(4)]
            idx += [2 * base + size - 1 - x for x in idx]
            vals = [ref[at(x), :] for x in idx]
            for k in range(4):
                exchange(vals, k, 4 + k)
            clean(vals, [0, 1, 2, 3], (2, 1))
            clean(vals, [7, 6, 5, 4], (2, 1))
            for x, v in zip(idx, vals):
                ref[at(x), :] = v
    tidy(ref, ref, count, step)


def tidy(src, dst, count, block):
    dists = []
    d = block // 2
    while d:
        dists.append(d)
        d //= 2
    for start in range(0, count, block):
        vals = [src[at(start + i), :] for i in range(block)]
        clean(vals, list(range(block)), dists)
        for i in range(block):
            dst[at(start + i), :] = vals[i]


def best_of(a, abase, b, bbase, tmp, dst, turn=0):
    step = TOPK // 8
    for i in range(step):
        vals = []
        for k in range(8):
            x = a[at(abase + i + step * k), :]
            y = b[at(bbase + TOPK - 1 - i - step * k), :]
            if turn:
                y = pltpu.roll(y, turn, 0)
            vals.append(jnp.maximum(x, y))
        clean(vals, list(range(8)), (4, 2, 1))
        for k in range(8):
            tmp[at(i + step * k), :] = vals[k]
    tidy(tmp, dst, TOPK, step)


def fused(
    rows, cap, q_ref, hot_hbm, cold_hbm, out_ref,
    hot_ref, cold_ref, list_sem, q_all, key, onehot, work, short, tmp, runs, hotbest, keep, pairbuf, sendbuf, mergebuf, recv,
    gs_sem, gr_sem, ps_sem, pr_sem, ss_sem, sr_sem,
):
    fetch_hot = pltpu.make_async_copy(hot_hbm, hot_ref, list_sem.at[0])
    fetch_cold = pltpu.make_async_copy(cold_hbm, cold_ref, list_sem.at[1])
    fetch_hot.start()
    fetch_cold.start()
    me = lax.axis_index("row")
    core = lax.rem(me, 2)
    partner = me + 1 - 2 * core
    across = me + 2 - 4 * lax.rem(me // 2, 2)
    hot_count, lsize = hot_ref.shape[0], hot_ref.shape[1]
    qcount = LANES
    nprobe = q_ref.shape[0] - qcount
    list_dev = cold_ref.shape[0]
    pack = LANES // cap
    groups = rows // pack
    f32 = jnp.float32

    def remote(src, dst, send_sem, recv_sem, to):
        return pltpu.make_async_remote_copy(
            src_ref=src, dst_ref=dst, send_sem=send_sem, recv_sem=recv_sem,
            device_id={"row": to}, device_id_type=pl.DeviceIdType.MESH,
        )

    def gather_copy(source, kind, step, to):
        src = q_ref if step == 0 and kind != 2 else q_all.at[source]
        return remote(src, q_all.at[source], gs_sem.at[kind, step], gr_sem.at[source], to)

    def line(step):
        return lax.rem(me + pack * step, rows)

    def column(step):
        return lax.rem(across + pack * step, rows)

    def arrived(source):
        gather_copy(source, 2, 0, partner).wait_recv()

    def relay_line(step):
        if step:
            arrived(line(step))
        gather_copy(line(step), 0, step, across).start()
        gather_copy(line(step), 1, step, partner).start()

    def relay_column(step):
        arrived(column(step))
        gather_copy(column(step), 2, step, partner).start()

    def pair_copy(step, k):
        return remote(
            sendbuf.at[step, 2 * k + 1 - core], pairbuf.at[step, k],
            ps_sem.at[step, k], pr_sem.at[step, k], partner,
        )

    def final_copy(step, k, to, source):
        return remote(
            mergebuf.at[step, 2 * k + core], recv.at[source], ss_sem.at[step, k], sr_sem.at[source], to
        )

    barrier = pltpu.get_barrier_semaphore()

    @pl.loop(1, rows)
    def _(d):
        pl.semaphore_signal(
            barrier, inc=1, device_id={"row": lax.rem(me + d, rows)},
            device_id_type=pl.DeviceIdType.MESH,
        )

    pl.semaphore_wait(barrier, rows - 1)

    relay_line(0)
    for step in range(1, groups):
        remote(
            q_ref, q_all.at[me], gs_sem.at[3, step], gr_sem.at[me], lax.rem(me + rows - pack * step, rows)
        ).start()
    q_all[me] = q_ref[...]

    before = (
        lax.broadcasted_iota(jnp.int32, (qcount, qcount), 0)
        < lax.broadcasted_iota(jnp.int32, (qcount, qcount), 1)
    )
    before = jnp.where(before, 1.0, 0.0).astype(jnp.bfloat16)

    def keys_of(pt, first, count):
        ids = (first + lax.broadcasted_iota(jnp.int32, (count, qcount), 0)).astype(f32)
        pt = pt.astype(f32)
        named = pt[0:1, :] == ids
        for j in range(1, nprobe):
            named = named | (pt[j : j + 1, :] == ids)
        ones = jnp.where(named, 1.0, 0.0)
        rank = jnp.dot(ones.astype(jnp.bfloat16), before, preferred_element_type=f32)
        return named, rank

    slot_row = lax.broadcasted_iota(jnp.int32, (LANES, pack * qcount), 0).astype(f32)
    lane = lax.broadcasted_iota(jnp.int32, (lsize, LANES), 1)

    def match(l):
        hit = slot_row == key[l : l + 1, :]
        hot1 = jnp.where(hit, 1.0, 0.0).astype(jnp.bfloat16)
        onehot[l] = hot1
        return hot1

    def spread(l, half):
        part = short[pl.ds(l, TOPK, stride=SUB), :]
        high = part.astype(jnp.bfloat16)
        low = (part - high.astype(f32)).astype(jnp.bfloat16)
        both = jnp.concatenate([high, low], axis=0)
        full = jnp.dot(both, onehot[l], preferred_element_type=f32)
        full = full[:TOPK, :] + full[TOPK:, :]
        full = jnp.where(key[l : l + 1, :] >= 0.0, full, LOW)
        for b in range(pack):
            runs[l // half, pl.ds((l % half) * pack + b, TOPK, stride=SUB), :] = full[
                :, b * qcount : (b + 1) * qcount
            ]

    def shorten():
        sort_runs(work, lsize)
        join_runs(work, lsize, 32)
        join_runs(work, lsize, 64)
        best_of(work, 0, work, TOPK, tmp, short)

    half = SUB // pack

    named, rank = keys_of(q_ref[qcount : qcount + nprobe, :qcount], 0, hot_count)
    for l in range(hot_count):
        value = jnp.where(named[l : l + 1, :], rank[l : l + 1, :] + float(cap * (l % pack)), -1.0)
        key[l // pack : l // pack + 1, (l % pack) * qcount : (l % pack + 1) * qcount] = value
    mine = q_ref[:qcount, :]
    stack = jnp.concatenate([mine] * pack, axis=0)
    fetch_hot.wait()
    for t in range(hot_count // pack):
        rows_t = jnp.dot(match(t), stack, preferred_element_type=f32).astype(jnp.bfloat16)
        score = None
        for c in range(pack):
            one = lax.dot_general(
                hot_ref[t * pack + c], rows_t, (((1,), (1,)), ((), ())), preferred_element_type=f32
            )
            score = one if score is None else jnp.where(lane >= c * cap, one, score)
        work[pl.ds(t, lsize, stride=SUB), :] = score
        work[pl.ds(hot_count // pack + t, lsize, stride=SUB), :] = score
    relay_column(0)
    shorten()
    relay_line(1)
    for t in range(hot_count // pack):
        spread(t, half)
    best_of(runs.at[0], 0, runs.at[1], 0, tmp, hotbest)
    relay_line(2)
    relay_column(1)
    fetch_cold.wait()

    def merge_out(step):
        g = lax.rem(me // pack + step, groups)
        for k in range(pack // 2):
            pair_copy(step, k).wait_recv()
            part = pairbuf[step, k]
            for c in range(2):
                runs[3, pl.ds(2 * k + c, TOPK, stride=SUB), :] = part
        best_of(keep.at[step], 0, runs.at[3], 0, tmp, runs.at[2])
        for b in range(pack):
            mergebuf[step, b] = runs[2, pl.ds(b, TOPK, stride=SUB), :]
        for k in range(pack // 2):
            to = g * pack + 2 * k + core

            @pl.when(to != me)
            def _():
                final_copy(step, k, to, me // 2).start()

            @pl.when(to == me)
            def _():
                recv[me // 2] = mergebuf[step, 2 * k + core]

    @pl.loop(0, groups)
    def _(step):
        g = lax.rem(me // pack + step, groups)
        arrived(lax.rem(partner + pack * step, rows))
        arrived(lax.rem(across + partner - me + pack * step, rows))
        for b in range(pack):
            block = g * pack + b
            named, rank = keys_of(
                q_all[block, qcount : qcount + nprobe, :qcount], hot_count + me * list_dev, list_dev
            )
            key[:, b * qcount : (b + 1) * qcount] = jnp.where(named, rank + float(cap * b), -1.0)
        stack = jnp.concatenate([q_all[g * pack + b, :qcount, :] for b in range(pack)], axis=0)
        for l in range(list_dev):
            match(l)
        every = jnp.dot(
            onehot[...].reshape(list_dev * LANES, pack * qcount), stack, preferred_element_type=f32
        ).astype(jnp.bfloat16)
        for l in range(list_dev):
            work[pl.ds(l, lsize, stride=SUB), :] = lax.dot_general(
                cold_ref[l], every[l * LANES : (l + 1) * LANES, :], (((1,), (1,)), ((), ())),
                preferred_element_type=f32,
            )

        @pl.when(step == 0)
        def _():
            relay_line(3)
            relay_column(2)

        shorten()

        @pl.when(step == 0)
        def _():
            relay_column(3)

        @pl.when(step >= 1)
        def _():
            merge_out(step - 1)

        for l in range(list_dev):
            spread(l, half)
        best_of(runs.at[0], 0, runs.at[1], 0, tmp, runs.at[0])
        best_of(runs.at[2], 0, runs.at[3], 0, tmp, runs.at[2])
        best_of(runs.at[0], 0, runs.at[2], 0, tmp, runs.at[0])
        best_of(runs.at[0], 0, runs.at[0], 0, tmp, keep.at[step], turn=pack)
        for b in range(pack):
            sendbuf[step, b] = keep[step, pl.ds(b, TOPK, stride=SUB), :]
        for k in range(pack // 2):
            pair_copy(step, k).start()

    merge_out(groups - 1)

    @pl.loop(1, rows // 2)
    def _(d):
        source = lax.rem(me // 2 + d, rows // 2)
        final_copy(0, 0, partner, source).wait_recv()

    for o in range(rows // 2):
        runs[0, pl.ds(o, TOPK, stride=SUB), :] = recv[o]
    best_of(hotbest, 0, runs.at[0], 0, tmp, hotbest)
    turn = SUB // 2
    src, dst = hotbest, runs.at[0]
    while turn:
        best_of(src, 0, src, 0, tmp, dst, turn=turn)
        src, dst = dst, src
        turn //= 2
    result = src[pl.ds(0, TOPK, stride=SUB), :]
    out_ref[...] = result.T

    for step in range(groups):
        gather_copy(line(step), 0, step, across).wait_send()
        gather_copy(line(step), 1, step, partner).wait_send()
        gather_copy(column(step), 2, step, partner).wait_send()
        if step:
            remote(q_ref, q_all.at[me], gs_sem.at[3, step], gr_sem.at[me], partner).wait_send()
        for k in range(pack // 2):
            pair_copy(step, k).wait_send()
            to = lax.rem(me // pack + step, groups) * pack + 2 * k + core

            @pl.when(to != me)
            def _():
                final_copy(step, k, to, me // 2).wait_send()


def shards(queries, probes, hot_lists, cold_lists):
    rows = lax.axis_size("row")
    qcount, nprobe = probes.shape
    list_dev = cold_lists.shape[0]
    hot_count, lsize, width = hot_lists.shape
    cap = 2 * ((qcount * nprobe + list_dev * rows - 1) // (list_dev * rows))
    pack = LANES // cap
    fits = (
        qcount == LANES and lsize == 2 * TOPK and list_dev == SUB and pack == 4
        and hot_count == pack * pack and rows == 2 * SUB and width >= qcount
        and hot_count + list_dev * rows <= 256
    )
    if not fits:
        return general(queries, probes, hot_lists, cold_lists)
    vmem = pl.BlockSpec(memory_space=pltpu.VMEM)
    far = pl.BlockSpec(memory_space=pl.ANY)
    dma = pltpu.SemaphoreType.DMA
    groups = rows // pack
    ids = jnp.pad(probes.T, ((0, 0), (0, width - qcount))).astype(jnp.bfloat16)
    held = jnp.concatenate([queries, ids], axis=0)
    run = pltpu.VMEM((TOPK * SUB, LANES), jnp.float32)
    return pl.pallas_call(
        functools.partial(fused, rows, cap),
        out_shape=jax.ShapeDtypeStruct((qcount, TOPK), jnp.float32),
        in_specs=[vmem, far, far],
        out_specs=vmem,
        scratch_shapes=[
            pltpu.VMEM(hot_lists.shape, jnp.bfloat16),
            pltpu.VMEM(cold_lists.shape, jnp.bfloat16),
            dma((2,)),
            pltpu.VMEM((rows,) + held.shape, jnp.bfloat16),
            pltpu.VMEM((list_dev, pack * qcount), jnp.float32),
            pltpu.VMEM((list_dev, LANES, pack * qcount), jnp.bfloat16),
            pltpu.VMEM((lsize * SUB, LANES), jnp.float32),
            run,
            run,
            pltpu.VMEM((list_dev * pack // SUB, TOPK * SUB, LANES), jnp.float32),
            run,
            pltpu.VMEM((groups, TOPK * SUB, LANES), jnp.float32),
            pltpu.VMEM((groups, pack // 2, TOPK, qcount), jnp.float32),
            pltpu.VMEM((groups, pack, TOPK, qcount), jnp.float32),
            pltpu.VMEM((groups, pack, TOPK, qcount), jnp.float32),
            pltpu.VMEM((rows // 2, TOPK, qcount), jnp.float32),
            dma((4, groups)),
            dma((rows,)),
            dma((groups, pack // 2)),
            dma((groups, pack // 2)),
            dma((groups, pack // 2)),
            dma((rows // 2,)),
        ],
        compiler_params=pltpu.CompilerParams(
            collective_id=0, has_side_effects=True, vmem_limit_bytes=60 * 1024 * 1024
        ),
    )(held, hot_lists, cold_lists)


def solution(mesh):
    placed = (
        P(("tenant", "row"), None),
        P(("tenant", "row"), None),
        P("tenant", None, None),
        P(("tenant", "row"), None, None),
    )
    return jax.shard_map(
        shards, mesh=mesh, in_specs=placed, out_specs=P(("tenant", "row"), None), check_vma=False
    )
```
